32 devices in a mesh: fsdp: 8 (over y, x, core), sp: 4 (over z).
Axes of the slice: x: 2, y: 2, z: 4, core: 2. Of those that a mesh axis runs over, the one named last changes fastest.
Arguments:
- query: bfloat16 [4096, 2048], P(('fsdp', 'sp')), may hold values from -6 to 6
- projected_key_rows: bfloat16 [4096, 2048], P(('fsdp', 'sp')), may hold values from -6 to 6
- value: bfloat16 [4096, 2048], P(('fsdp', 'sp')), may hold values from -6 to 6
- blocks: int32 [8, 4, 6], P('fsdp'), may hold values from 0 to 3, as said below
- frozen_output_weight: bfloat16 [2048, 2048], P('fsdp'), may hold values from -0.125 to 0.125
- adapter_down_weight: bfloat16 [2048, 64], P('fsdp'), may hold values from -0.125 to 0.125
- adapter_up_weight_transposed: bfloat16 [2048, 64], P('fsdp'), may hold values from -0.75 to 0.75
- cotangent: bfloat16 [4096, 2048], P(('fsdp', 'sp')), may hold values from -6 to 6
Outputs:
- mixed: bfloat16 [4096, 2048], P(('fsdp', 'sp'))
- grad_query: bfloat16 [4096, 2048], P(('fsdp', 'sp'))
- grad_key: bfloat16 [4096, 2048], P(('fsdp', 'sp'))
- grad_value: bfloat16 [4096, 2048], P(('fsdp', 'sp'))
- grad_down: float32 [2048, 64], P('fsdp')
- grad_up: float32 [2048, 64], P('fsdp')
The draws below stay inside these ranges and needn't reach their ends.
Inputs may be any that keep to these rules, and one draw needn't show every extreme that they name: Entry 1 of each list is the query block itself, entries 0 and 2 its neighbours (wrapping at the ends), entry 3 one block common to all query blocks of the sequence, the rest any blocks.
All inputs are finite; a program needn't handle non-finite values.
Results may differ from the reference program's by a relative error of at most 0.0081.
Values may be sent and summed in bfloat16 or wider, within the bound.
No kernel may reach another device: no remote copies, remote signals or barrier semaphores. Data moves between devices by JAX's collectives and lax.ppermute only.
A program may use at most 128 MiB of HBM per device.

```python
import math
import jax
import jax.numpy as jnp
from jax import lax

MODEL_WIDTH = 2048
HEADS = 16
BLOCK = 128
KEY_BLOCKS = 6
ADAPTER_RANK = 64
NBLOCKS = 4
SEQS = 8
TOKENS = 4096


def drawn_pair(key):
    first = jnp.clip(jax.random.normal(jax.random.fold_in(key, 101), (TOKENS, MODEL_WIDTH), jnp.float32), -6.0, 6.0)
    second = jnp.clip(jax.random.normal(jax.random.fold_in(key, 202), (TOKENS, MODEL_WIDTH), jnp.float32), -6.0, 6.0)
    return (first, second)


def draw_query(key, part):
    return drawn_pair(key)[0].astype(jnp.bfloat16)


def draw_projected_key_rows(key, part):
    return drawn_pair(key)[1].astype(jnp.bfloat16)


def draw_blocks(key, part):
    count = NBLOCKS
    index_row = jnp.arange(count, dtype=jnp.int32)
    window = jnp.stack([(index_row - 1) % count, index_row, (index_row + 1) % count], axis=-1)
    window = jnp.broadcast_to(window[None, :, :], (SEQS, count, 3))
    common = jax.random.randint(jax.random.fold_in(key, 404), (SEQS, 1, 1), 0, count, dtype=jnp.int32)
    common = jnp.broadcast_to(common, (SEQS, count, 1))
    random_part = jax.random.randint(jax.random.fold_in(key, 505), (SEQS, count, KEY_BLOCKS - 4), 0, count, dtype=jnp.int32)
    return jnp.concatenate([window, common, random_part], axis=-1).astype(jnp.int32)


def with_spikes(values, rng, source, target, blocks, factor):
    def block_of(dim):
        return (jnp.arange(values.shape[dim]) // (values.shape[dim] // blocks)).reshape((-1,) + (1,) * (values.ndim - 1 - dim))

    first = jax.random.permutation(rng, blocks)[block_of(target)]
    other_side = (block_of(target) + blocks // 2) % blocks
    return jnp.where((block_of(source) == first) | (block_of(source) == other_side), factor * values, values)


def block_levels(key, extent, split, least, top_value):
    gain = 1.0
    for position, shards_of in split:
        steps = jax.random.uniform(jax.random.fold_in(jax.random.fold_in(key, 6), position), (shards_of,), jnp.float32, least / len(split), top_value / len(split))
        gain = gain * jnp.repeat(jnp.exp(steps), extent[position] // shards_of).reshape((-1,) + (1,) * (len(extent) - 1 - position))
    return gain


def noise(rng, shape, scale, most, pieces=(), kind=jnp.bfloat16):
    entries = jax.random.normal(rng, shape, jnp.float32) * scale
    if len(pieces) > 0:
        entries = block_levels(rng, shape, pieces, -0.22, 0.18) * entries
    return jnp.clip(entries, min=-most, max=most).astype(kind)


def bell_draw_with(rng, dims, spread, most, pieces, heavy, held_as=jnp.bfloat16):
    drawn = spread * jax.random.normal(rng, dims, jnp.float32)
    if pieces:
        drawn = drawn * block_levels(rng, dims, pieces, -0.22, 0.18)
    return jnp.clip(with_spikes(drawn, jax.random.fold_in(rng, 3), *heavy), -most, most).astype(held_as)


def setup_inputs(seed: int = 0) -> dict:
    key_list = jax.random.split(jax.random.key(seed), 9)
    return {
        "query": draw_query(jax.random.fold_in(key_list[8], 71), 0),
        "projected_key_rows": draw_projected_key_rows(jax.random.fold_in(key_list[8], 71), 0),
        "value": noise(key_list[2], (TOKENS, MODEL_WIDTH), 1.0, 6.0, ((0, 32),)),
        "blocks": draw_blocks(jax.random.fold_in(key_list[8], 71), 0),
        "frozen_output_weight": noise(key_list[4], (MODEL_WIDTH, MODEL_WIDTH), MODEL_WIDTH ** -0.5, 0.125, ((0, 8),)),
        "adapter_down_weight": noise(key_list[5], (MODEL_WIDTH, ADAPTER_RANK), MODEL_WIDTH ** -0.5, 0.125, ((0, 8),)),
        "adapter_up_weight_transposed": noise(key_list[6], (MODEL_WIDTH, ADAPTER_RANK), ADAPTER_RANK ** -0.5, 0.75, ((0, 8),)),
        "cotangent": bell_draw_with(key_list[7], (TOKENS, MODEL_WIDTH), 1.0, 6.0, ((0, 32),), (0, 1, 32, 2.75)),
    }


def attend_sequence(query, projected_key_rows, value, lists):
    count = lists.shape[0]
    head_dim = MODEL_WIDTH // HEADS
    scaling = 1.0 / math.sqrt(head_dim)
    query_blocks = query.astype(jnp.float32).reshape(count, BLOCK, HEADS, head_dim)
    key_blocks = projected_key_rows.astype(jnp.float32).reshape(count, BLOCK, HEADS, head_dim)
    value_blocks = value.astype(jnp.float32).reshape(count, BLOCK, HEADS, head_dim)
    listed = lists.reshape(-1).astype(jnp.int32)
    keys_gathered = jnp.take(key_blocks, listed, axis=0).reshape(count, KEY_BLOCKS * BLOCK, HEADS, head_dim)
    values_gathered = jnp.take(value_blocks, listed, axis=0).reshape(count, KEY_BLOCKS * BLOCK, HEADS, head_dim)
    scores = jnp.einsum('gqhd,gkhd->ghqk', query_blocks, keys_gathered) * scaling
    highest = lax.optimization_barrier(jnp.max(scores, axis=-1, keepdims=True))
    raised = jnp.exp(scores - highest)
    probs = raised / lax.optimization_barrier(jnp.sum(raised, axis=-1, keepdims=True))
    weights = probs.astype(jnp.bfloat16)
    attended_context = jnp.einsum('ghqk,gkhd->gqhd', weights.astype(jnp.float32), values_gathered).astype(jnp.bfloat16)
    return (attended_context.reshape(count * BLOCK, MODEL_WIDTH), probs, weights, keys_gathered, values_gathered, query_blocks)

def attend_backward(query, projected_key_rows, value, lists, attended_context_gradient):
    count = lists.shape[0]
    head_dim = MODEL_WIDTH // HEADS
    scaling = 1.0 / math.sqrt(head_dim)
    unused, probs, weights, keys_gathered, values_gathered, query_blocks = attend_sequence(query, projected_key_rows, value, lists)
    grad_blocks = attended_context_gradient.astype(jnp.float32).reshape(count, BLOCK, HEADS, head_dim)
    dweights = jnp.einsum('gqhd,gkhd->ghqk', grad_blocks, values_gathered)
    correction = lax.optimization_barrier(jnp.sum(probs * dweights, axis=-1, keepdims=True))
    dscores = (probs * (dweights - correction) * scaling).astype(jnp.bfloat16)
    grad_query = jnp.einsum('ghqk,gkhd->gqhd', dscores.astype(jnp.float32), keys_gathered).astype(jnp.bfloat16)
    key_terms = jnp.einsum('ghqk,gqhd->gkhd', dscores.astype(jnp.float32), query_blocks)
    value_terms = jnp.einsum('ghqk,gqhd->gkhd', weights.astype(jnp.float32), grad_blocks)
    listed = lists.reshape(-1).astype(jnp.int32)
    one_hot = (listed[:, None] == jnp.arange(count, dtype=jnp.int32)[None, :]).astype(jnp.float32)
    grad_key = jnp.einsum('in,ij->nj', one_hot, key_terms.reshape(count * KEY_BLOCKS, BLOCK * MODEL_WIDTH), precision=lax.Precision.HIGHEST)
    grad_value = jnp.einsum('in,ij->nj', one_hot, value_terms.reshape(count * KEY_BLOCKS, BLOCK * MODEL_WIDTH), precision=lax.Precision.HIGHEST)
    return (grad_query.reshape(count * BLOCK, MODEL_WIDTH), grad_key.reshape(count * BLOCK, MODEL_WIDTH).astype(jnp.bfloat16), grad_value.reshape(count * BLOCK, MODEL_WIDTH).astype(jnp.bfloat16))

def reference(query, projected_key_rows, value, blocks, frozen_output_weight, adapter_down_weight, adapter_up_weight_transposed, cotangent):
    sequences = blocks.shape[0]
    length = query.shape[0] // sequences

    def shaped(array):
        return array.reshape(sequences, length, MODEL_WIDTH)
    attended_context = lax.map(lambda items: attend_sequence(items[0], items[1], items[2], items[3])[0], (shaped(query), shaped(projected_key_rows), shaped(value), blocks)).reshape(-1, MODEL_WIDTH)
    reduced_rank_output = jnp.dot(attended_context, adapter_down_weight, preferred_element_type=jnp.float32).astype(jnp.bfloat16)
    mixed = (jnp.dot(attended_context, frozen_output_weight, preferred_element_type=jnp.float32) + jnp.dot(reduced_rank_output, adapter_up_weight_transposed.T, preferred_element_type=jnp.float32)).astype(jnp.bfloat16)
    reduced_gradient = jnp.dot(cotangent, adapter_up_weight_transposed, preferred_element_type=jnp.float32).astype(jnp.bfloat16)
    attended_context_gradient = (jnp.dot(cotangent, frozen_output_weight.T, preferred_element_type=jnp.float32) + jnp.dot(reduced_gradient, adapter_down_weight.T, preferred_element_type=jnp.float32)).astype(jnp.bfloat16)
    normal_factor = 1.0 / math.sqrt(TOKENS)
    grad_down = jnp.dot(attended_context.T, reduced_gradient, preferred_element_type=jnp.float32) * normal_factor
    grad_up = jnp.dot(cotangent.T, reduced_rank_output, preferred_element_type=jnp.float32) * normal_factor
    grad_query, grad_key, grad_value = lax.map(lambda items: attend_backward(items[0], items[1], items[2], items[3], items[4]), (shaped(query), shaped(projected_key_rows), shaped(value), blocks, shaped(attended_context_gradient)))
    return (mixed, grad_query.reshape(-1, MODEL_WIDTH), grad_key.reshape(-1, MODEL_WIDTH), grad_value.reshape(-1, MODEL_WIDTH), grad_down, grad_up)
```

```python
import functools
import math

import jax
import jax.numpy as jnp
from jax import lax
from jax.experimental import pallas as pl
from jax.experimental.pallas import tpu as pltpu
from jax.sharding import PartitionSpec as P

MODEL_WIDTH = 2048
HEADS = 16
BLOCK = 128
KEY_BLOCKS = 6
ADAPTER_RANK = 64
HEAD_DIM = MODEL_WIDTH // HEADS
SCALING = 1.0 / math.sqrt(HEAD_DIM)
EXPONENT = SCALING * math.log2(math.e)
ABSENT = 1e30
VMEM_LIMIT = 60 * 1024 * 1024


SMEM = pl.BlockSpec(memory_space=pltpu.SMEM)
VMEM = pl.BlockSpec(memory_space=pltpu.VMEM)
ANY = pl.BlockSpec(memory_space=pl.ANY)
BF16 = jnp.bfloat16
F32 = jnp.float32


def struct(shape, dtype=BF16):
    return jax.ShapeDtypeStruct(shape, dtype)


def cost(flops, moved, exps=0):
    return pl.CostEstimate(flops=int(flops), bytes_accessed=int(moved), transcendentals=int(exps))


def product(a, b, da, db):
    return lax.dot_general(a, b, (((da,), (db,)), ((), ())), preferred_element_type=F32)


def pack_kernel(span, chunks, place_ref, *refs):
    sources = refs[:3]
    outs = refs[3 : 3 + span * chunks]
    in_sems, out_sems, buffers = refs[3 + span * chunks :]
    width = MODEL_WIDTH // span // chunks
    place = place_ref[0]
    copies = []
    for index in range(span * chunks):
        chunk, shift = divmod(index, span)
        group = lax.rem(place + shift, span)
        start = pl.multiple_of(group * (width * chunks) + chunk * width, width)
        for array in range(3):
            copy = pltpu.make_async_copy(
                sources[array].at[:, pl.ds(start, width)],
                buffers.at[index, array],
                in_sems.at[index, array],
            )
            copy.start()
            copies.append(copy)
    pushes = []
    for index in range(span * chunks):
        for array in range(3):
            copies[3 * index + array].wait()
        push = pltpu.make_async_copy(buffers.at[index], outs[index], out_sems.at[index])
        push.start()
        pushes.append(push)
    for push in pushes:
        push.wait()


def pack(place, arrays, span, chunks):
    width = MODEL_WIDTH // span // chunks
    count = span * chunks
    moved = 2 * 3 * BLOCK * MODEL_WIDTH * 2
    outs = pl.pallas_call(
        functools.partial(pack_kernel, span, chunks),
        name="pack",
        out_shape=[struct((3, BLOCK, width))] * count,
        in_specs=[SMEM] + [ANY] * 3,
        out_specs=[ANY] * count,
        scratch_shapes=[
            pltpu.SemaphoreType.DMA((count, 3)),
            pltpu.SemaphoreType.DMA((count,)),
            pltpu.VMEM((count, 3, BLOCK, width), BF16),
        ],
        compiler_params=pltpu.CompilerParams(vmem_limit_bytes=VMEM_LIMIT),
        cost_estimate=cost(0, moved),
    )(place, *arrays)
    return [outs[c * span : (c + 1) * span] for c in range(chunks)]


def unpack_kernel(span, chunks, place_ref, *refs):
    pieces = refs[: span * chunks]
    outs = refs[span * chunks : span * chunks + 3]
    in_sems, out_sems, buffers = refs[span * chunks + 3 :]
    width = MODEL_WIDTH // span // chunks
    place = place_ref[0]
    pulls = []
    for index in range(span * chunks):
        pull = pltpu.make_async_copy(pieces[index], buffers.at[index], in_sems.at[index])
        pull.start()
        pulls.append(pull)
    pushes = []
    for index in range(span * chunks):
        chunk, shift = divmod(index, span)
        group = lax.rem(place + shift, span)
        start = pl.multiple_of(group * (width * chunks) + chunk * width, width)
        pulls[index].wait()
        for array in range(3):
            push = pltpu.make_async_copy(
                buffers.at[index, array],
                outs[array].at[:, pl.ds(start, width)],
                out_sems.at[index, array],
            )
            push.start()
            pushes.append(push)
    for push in pushes:
        push.wait()


def unpack(place, pieces, span, chunks):
    width = MODEL_WIDTH // span // chunks
    count = span * chunks
    flat = [piece for chunk in pieces for piece in chunk]
    return pl.pallas_call(
        functools.partial(unpack_kernel, span, chunks),
        name="unpack",
        out_shape=[struct((BLOCK, MODEL_WIDTH))] * 3,
        in_specs=[SMEM] + [ANY] * count,
        out_specs=[ANY] * 3,
        scratch_shapes=[
            pltpu.SemaphoreType.DMA((count,)),
            pltpu.SemaphoreType.DMA((count, 3)),
            pltpu.VMEM((count, 3, BLOCK, width), BF16),
        ],
        compiler_params=pltpu.CompilerParams(vmem_limit_bytes=VMEM_LIMIT),
        cost_estimate=cost(0, 2 * 3 * BLOCK * MODEL_WIDTH * 2),
    )(place, *flat)


def listed_counts(place, lists_ref, span):
    counts = []
    for a in range(span):
        row = lax.rem(place - a + span, span)
        entries = [lists_ref[row, e] for e in range(KEY_BLOCKS)]
        counts.append(
            [
                sum(
                    jnp.where(entry == lax.rem(place - c + span, span), 1.0, 0.0)
                    for entry in entries
                )
                for c in range(span)
            ]
        )
    return counts


def lane_rows(values):
    return jnp.concatenate([jnp.full((1, BLOCK), value, F32) for value in values], axis=1)


def group_probs(keys, queries, offsets, span):
    scores = product(keys, queries, 1, 1)
    tops = [
        jnp.max(scores[c * BLOCK : (c + 1) * BLOCK], axis=0, keepdims=True) * EXPONENT
        for c in range(span)
    ]
    highest = functools.reduce(
        jnp.maximum,
        [jnp.where(offsets[c] > -ABSENT, tops[c], -ABSENT) for c in range(span)],
    )
    raised = []
    total = None
    for c in range(span):
        part = jnp.exp2(scores[c * BLOCK : (c + 1) * BLOCK] * EXPONENT + (offsets[c] - highest))
        raised.append(part)
        part_sum = jnp.sum(part, axis=0, keepdims=True)
        total = part_sum if total is None else total + part_sum
    inverse = 1.0 / total
    return [part * inverse for part in raised]


def block_offsets(counts, blocks_of_group, span):
    rows = []
    for c in range(span):
        listed = lane_rows([counts[a][c] for a in blocks_of_group])
        rows.append(jnp.where(listed > 0.0, jnp.log2(jnp.maximum(listed, 1.0)), -ABSENT))
    return rows


def groups_of(span):
    size = 2 if span % 2 == 0 else 1
    return [list(range(start, start + size)) for start in range(0, span, size)]


def forward_kernel(span, heads, place_ref, lists_ref, *refs):
    pieces, outs = refs[:span], refs[span:]
    place = place_ref[0]
    counts = listed_counts(place, lists_ref, span)
    groups = groups_of(span)
    offsets = [block_offsets(counts, group, span) for group in groups]
    for h in range(heads):
        lanes = slice(h * HEAD_DIM, (h + 1) * HEAD_DIM)
        keys = jnp.concatenate([piece[1, :, lanes] for piece in pieces], axis=0)
        values = jnp.concatenate([piece[2, :, lanes] for piece in pieces], axis=0)
        for group, offset in zip(groups, offsets):
            queries = jnp.concatenate([pieces[a][0, :, lanes] for a in group], axis=0)
            probs = group_probs(keys, queries, offset, span)
            weights = jnp.concatenate([part.astype(BF16) for part in probs], axis=0)
            context = product(weights, values, 0, 0).astype(BF16)
            for place_in_group, a in enumerate(group):
                outs[a][:, lanes] = context[
                    place_in_group * BLOCK : (place_in_group + 1) * BLOCK
                ]


def attention_forward(place, lists, pieces, span):
    width = pieces[0].shape[2]
    heads = width // HEAD_DIM
    tile = (span * BLOCK) ** 2 * heads
    return pl.pallas_call(
        functools.partial(forward_kernel, span, heads),
        name="attend",
        out_shape=[struct((BLOCK, width))] * span,
        in_specs=[SMEM, SMEM] + [VMEM] * span,
        out_specs=[VMEM] * span,
        compiler_params=pltpu.CompilerParams(vmem_limit_bytes=VMEM_LIMIT),
        cost_estimate=cost(4 * tile * HEAD_DIM, 4 * span * BLOCK * width * 2, tile),
    )(place, lists, *pieces)


def backward_kernel(span, heads, place_ref, lists_ref, *refs):
    pieces, grads, outs = refs[:span], refs[span : 2 * span], refs[2 * span :]
    place = place_ref[0]
    counts = listed_counts(place, lists_ref, span)
    groups = groups_of(span)
    offsets = [block_offsets(counts, group, span) for group in groups]
    for h in range(heads):
        lanes = slice(h * HEAD_DIM, (h + 1) * HEAD_DIM)
        keys = jnp.concatenate([piece[1, :, lanes] for piece in pieces], axis=0)
        values = jnp.concatenate([piece[2, :, lanes] for piece in pieces], axis=0)
        key_total, value_total = None, None
        for group, offset in zip(groups, offsets):
            queries = jnp.concatenate([pieces[a][0, :, lanes] for a in group], axis=0)
            slopes = jnp.concatenate([grads[a][:, lanes] for a in group], axis=0)
            probs = group_probs(keys, queries, offset, span)
            dweights = product(values, slopes, 1, 1)
            parts = [dweights[c * BLOCK : (c + 1) * BLOCK] for c in range(span)]
            correction = functools.reduce(
                jnp.add,
                [jnp.sum(p * d, axis=0, keepdims=True) for p, d in zip(probs, parts)],
            )
            weights = jnp.concatenate([part.astype(BF16) for part in probs], axis=0)
            dscores = jnp.concatenate(
                [
                    (p * (d - correction) * SCALING).astype(BF16)
                    for p, d in zip(probs, parts)
                ],
                axis=0,
            )
            key_part = product(dscores, queries, 1, 0)
            value_part = product(weights, slopes, 1, 0)
            key_total = key_part if key_total is None else key_total + key_part
            value_total = value_part if value_total is None else value_total + value_part
            query_part = product(dscores, keys, 0, 0).astype(BF16)
            for place_in_group, a in enumerate(group):
                outs[a][0, :, lanes] = query_part[
                    place_in_group * BLOCK : (place_in_group + 1) * BLOCK
                ]
        for a in range(span):
            outs[a][1, :, lanes] = key_total[a * BLOCK : (a + 1) * BLOCK].astype(BF16)
            outs[a][2, :, lanes] = value_total[a * BLOCK : (a + 1) * BLOCK].astype(BF16)


def attention_backward(place, lists, pieces, grads, span):
    width = pieces[0].shape[2]
    heads = width // HEAD_DIM
    tile = (span * BLOCK) ** 2 * heads
    return pl.pallas_call(
        functools.partial(backward_kernel, span, heads),
        name="attend_backward",
        out_shape=[struct((3, BLOCK, width))] * span,
        in_specs=[SMEM, SMEM] + [VMEM] * (2 * span),
        out_specs=[VMEM] * span,
        compiler_params=pltpu.CompilerParams(vmem_limit_bytes=VMEM_LIMIT),
        cost_estimate=cost(10 * tile * HEAD_DIM, 7 * span * BLOCK * width * 2, tile),
    )(place, lists, *pieces, *grads)


def pair_exchange(array, distance, size):
    return lax.ppermute(array, "fsdp", [(i, i ^ distance) for i in range(size)])


def gather_pieces(rows):
    half = rows.shape[0] // 2
    swap = functools.partial(pair_exchange, size=8)
    along_x = swap(rows, 2)
    along_y = swap(rows, 4)
    first = swap(along_y[:half], 2)
    second = swap(along_x[half:], 4)
    near = [(0, 0, rows), (2, 0, along_x), (4, 0, along_y), (6, 0, first), (6, half, second)]
    return near + [(d ^ 1, start, swap(array, 1)) for d, start, array in near]


def load_weights(pieces, refs, own, scratch, sems):
    total = scratch.shape[0]
    rows = total // 8
    copies = []
    for index, (distance, start) in enumerate(pieces):
        size = refs[index].shape[0]
        first = pl.multiple_of((own ^ distance) * rows + start, size)
        copy = pltpu.make_async_copy(
            refs[index], scratch.at[pl.ds(first, size), :], sems.at[index]
        )
        copy.start()
        copies.append(copy)
    return copies


def dcontext_kernel(pieces, span, chunks, spots_ref, cot_ref, *refs):
    count = len(pieces)
    weight_refs = refs[:count]
    outs = refs[count : count + span * chunks]
    dlow_ref, scratch, sems = refs[count + span * chunks :]
    place, own = spots_ref[0], spots_ref[1]
    for copy in load_weights(pieces, weight_refs, own, scratch, sems):
        copy.wait()
    cot = cot_ref[...]
    down = scratch[:, MODEL_WIDTH : MODEL_WIDTH + ADAPTER_RANK]
    up = scratch[:, MODEL_WIDTH + ADAPTER_RANK :]
    dlow = product(cot, up, 1, 0).astype(BF16)
    dlow_ref[...] = dlow
    width = MODEL_WIDTH // span // chunks
    for index in range(span * chunks):
        chunk, shift = divmod(index, span)
        group = lax.rem(place + shift, span)
        start = pl.multiple_of(group * (width * chunks) + chunk * width, width)
        rows = pl.ds(start, width)
        outs[index][...] = (
            product(cot, scratch[rows, :MODEL_WIDTH], 1, 1)
            + product(dlow, scratch[rows, MODEL_WIDTH : MODEL_WIDTH + ADAPTER_RANK], 1, 1)
        ).astype(BF16)


def mixed_kernel(pieces, span, chunks, spots_ref, cot_ref, dlow_ref, *refs):
    count = len(pieces)
    weight_refs = refs[:count]
    context_refs = refs[count : count + span * chunks]
    mixed_ref, terms_ref, scratch, context_buffer, sems = refs[count + span * chunks :]
    place, own = spots_ref[0], spots_ref[1]
    copies = load_weights(pieces, weight_refs, own, scratch, sems)
    width = MODEL_WIDTH // span // chunks
    for index in range(span * chunks):
        chunk, shift = divmod(index, span)
        group = lax.rem(place + shift, span)
        start = pl.multiple_of(group * (width * chunks) + chunk * width, width)
        context_buffer[:, pl.ds(start, width)] = context_refs[index][...]
    context = context_buffer[...]
    for copy in copies:
        copy.wait()
    down = scratch[:, MODEL_WIDTH : MODEL_WIDTH + ADAPTER_RANK]
    low = product(context, down, 1, 0).astype(BF16)
    dlow = dlow_ref[...]
    tile = MODEL_WIDTH // 8
    factor = 1.0 / math.sqrt(8 * span * BLOCK)
    for index in range(8):
        lanes = slice(index * tile, (index + 1) * tile)
        mixed_ref[:, lanes] = (
            product(context, scratch[:, lanes], 1, 0)
            + product(low, scratch[lanes, MODEL_WIDTH + ADAPTER_RANK :], 1, 1)
        ).astype(BF16)
        terms_ref[index, :ADAPTER_RANK, :] = (
            product(dlow, context[:, lanes], 0, 0) * factor
        ).astype(BF16)
        terms_ref[index, ADAPTER_RANK:, :] = (
            product(low, cot_ref[:, lanes], 0, 0) * factor
        ).astype(BF16)


def weight_call(kernel, name, pieces, span, chunks, out_shape, ins, spots, extra_scratch):
    labels = [(distance, start) for distance, start, unused in pieces]
    arrays = [array for unused, start, array in pieces]
    flops = 2 * BLOCK * MODEL_WIDTH * (MODEL_WIDTH + 2 * ADAPTER_RANK)
    lead, tail = ins
    return pl.pallas_call(
        functools.partial(kernel, labels, span, chunks),
        name=name,
        out_shape=out_shape,
        in_specs=[SMEM] + [VMEM] * len(lead) + [ANY] * len(arrays) + [VMEM] * len(tail),
        out_specs=[VMEM] * len(out_shape),
        scratch_shapes=[pltpu.VMEM((MODEL_WIDTH, MODEL_WIDTH + 2 * ADAPTER_RANK), BF16)]
        + extra_scratch
        + [pltpu.SemaphoreType.DMA((len(arrays),))],
        compiler_params=pltpu.CompilerParams(vmem_limit_bytes=VMEM_LIMIT),
        cost_estimate=cost(flops, MODEL_WIDTH * MODEL_WIDTH * 2),
    )(spots, *lead, *arrays, *tail)


def shifted(array, span, shift):
    if shift % span == 0:
        return array
    return lax.ppermute(array, "sp", [(i, (i + shift) % span) for i in range(span)])


def shards(
    chunks,
    query,
    projected_key_rows,
    value,
    blocks,
    frozen_output_weight,
    adapter_down_weight,
    adapter_up_weight_transposed,
    cotangent,
):
    span = lax.axis_size("sp")
    parts = lax.axis_size("fsdp")
    place = lax.axis_index("sp").astype(jnp.int32)
    own = lax.axis_index("fsdp").astype(jnp.int32)
    place_row = place.reshape(1)
    lists = blocks[0]
    paired = parts == 8
    width = MODEL_WIDTH // span // chunks

    weight_rows = jnp.concatenate(
        [frozen_output_weight, adapter_down_weight, adapter_up_weight_transposed], axis=1
    )
    sent = pack(place_row, (query, projected_key_rows, value), span, chunks)
    if paired:
        weights = gather_pieces(weight_rows)
    else:
        gathered = lax.all_gather(weight_rows, "fsdp", axis=0, tiled=True)
        full_out = gathered[:, :MODEL_WIDTH]
        full_down = gathered[:, MODEL_WIDTH : MODEL_WIDTH + ADAPTER_RANK]
        full_up = gathered[:, MODEL_WIDTH + ADAPTER_RANK :]
    heads_in = [
        [shifted(piece, span, shift) for shift, piece in enumerate(chunk)] for chunk in sent
    ]

    def columns(array):
        grouped = jnp.roll(array.reshape(BLOCK, span, chunks * width), -place, axis=1)
        return [
            [grouped[:, shift, c * width : (c + 1) * width] for shift in range(span)]
            for c in range(chunks)
        ]

    def joined(nested):
        stacked = jnp.stack(
            [
                jnp.concatenate([nested[c][shift] for c in range(chunks)], axis=-1)
                for shift in range(span)
            ],
            axis=1,
        )
        return jnp.roll(stacked, place, axis=1).reshape(BLOCK, MODEL_WIDTH)

    spots = jnp.stack([place, own])
    if paired:
        *dcontext, dlow = weight_call(
            dcontext_kernel,
            "dcontext",
            weights,
            span,
            chunks,
            [struct((BLOCK, width))] * (span * chunks) + [struct((BLOCK, ADAPTER_RANK))],
            ((cotangent,), ()),
            spots,
            [],
        )
        dcontext = [dcontext[c * span : (c + 1) * span] for c in range(chunks)]
    else:
        dlow = jnp.dot(cotangent, full_up, preferred_element_type=F32).astype(BF16)
        dcontext = columns(
            (
                jnp.einsum("td,ed->te", cotangent, full_out, preferred_element_type=F32)
                + jnp.einsum("tr,er->te", dlow, full_down, preferred_element_type=F32)
            ).astype(BF16)
        )
    grads_in = [
        [shifted(piece, span, shift) for shift, piece in enumerate(chunk)] for chunk in dcontext
    ]
    context_heads = [attention_forward(place_row, lists, chunk, span) for chunk in heads_in]
    context = [
        [shifted(piece, span, -shift) for shift, piece in enumerate(chunk)]
        for chunk in context_heads
    ]
    grad_heads = [
        attention_backward(place_row, lists, chunk, grads, span)
        for chunk, grads in zip(heads_in, grads_in)
    ]
    grads_out = [
        [shifted(piece, span, -shift) for shift, piece in enumerate(chunk)]
        for chunk in grad_heads
    ]
    tile = MODEL_WIDTH // parts
    if paired:
        mixed, terms = weight_call(
            mixed_kernel,
            "mixed",
            weights,
            span,
            chunks,
            [struct((BLOCK, MODEL_WIDTH)), struct((8, 2 * ADAPTER_RANK, tile))],
            ((cotangent, dlow), [piece for chunk in context for piece in chunk]),
            spots,
            [pltpu.VMEM((BLOCK, MODEL_WIDTH), BF16)],
        )
    else:
        rows = joined(context)
        low = jnp.dot(rows, full_down, preferred_element_type=F32).astype(BF16)
        mixed = (
            jnp.dot(rows, full_out, preferred_element_type=F32)
            + jnp.einsum("tr,dr->td", low, full_up, preferred_element_type=F32)
        ).astype(BF16)
        factor = 1.0 / math.sqrt(parts * span * BLOCK)
        terms = jnp.concatenate(
            [
                jnp.einsum("tr,td->rd", dlow, rows, preferred_element_type=F32),
                jnp.einsum("tr,td->rd", low, cotangent, preferred_element_type=F32),
            ],
            axis=0,
        )
        terms = (terms * factor).astype(BF16).reshape(2 * ADAPTER_RANK, parts, tile)
        terms = terms.transpose(1, 0, 2)
    received = lax.all_to_all(terms, "fsdp", split_axis=0, concat_axis=0)
    own_sum = jnp.sum(received.astype(F32), axis=0).astype(BF16)
    total = own_sum.astype(F32)
    for shift in range(1, span):
        total = total + shifted(own_sum, span, shift).astype(F32)
    total = total.T
    grad_down = total[:, :ADAPTER_RANK]
    grad_up = total[:, ADAPTER_RANK:]
    grad_query, grad_key, grad_value = unpack(place_row, grads_out, span, chunks)
    return (mixed, grad_query, grad_key, grad_value, grad_down, grad_up)


def solution(mesh):
    rows = P(("fsdp", "sp"), None)
    weight = P("fsdp", None)
    in_specs = (rows, rows, rows, P("fsdp", None, None), weight, weight, weight, rows)
    out_specs = (rows, rows, rows, rows, weight, weight)
    heads = HEADS // mesh.shape["sp"]
    chunks = 1
    body = functools.partial(shards, min(chunks, heads))
    return jax.shard_map(body, mesh=mesh, in_specs=in_specs, out_specs=out_specs, check_vma=False)
```
